32 devices in a mesh: segment: 4 (over y, x), tok: 8 (over z, core).
Axes of the slice: x: 2, y: 2, z: 4, core: 2. Of those that a mesh axis runs over, the one named last changes fastest.
Arguments:
- inputs: bfloat16 [2, 16, 8192], P(None, 'tok'), may hold values from -6 to 6
- weights: bfloat16 [4, 8192, 8192], P('segment', None, 'tok'), may hold values from -0.09375 to 0.09375
- keep_mask: int32 [4, 64, 64], P('segment', None, 'tok'), may hold values 0 or 1
- gains: float32 [4, 8192], P('segment'), may hold values from 0.1 to 1.9
Outputs:
- acts: bfloat16 [4, 2, 16, 8192], P('segment', None, 'tok')
- factors: float32 [4, 1024, 1024], P('segment')
The draws below stay inside these ranges and needn't reach their ends.
All inputs are finite; a program needn't handle non-finite values. No bound on the sum of `keep_mask` on one device may be relied on, other than what follows from the above.
Results may differ from the reference program's by a relative error of at most 0.0072.
Values may be sent and summed in bfloat16 or wider, within the bound.
A program may use at most 128 MiB of HBM per device.

```python
import jax
import jax.numpy as jnp
from jax import lax

D = 8192
BLK = 128
GRP = 1024
MICRO = 2
TOKENS = 16
N_SEGMENT = 4


def place_ends(result, key, low, largest):
    spot = [jax.random.randint(jax.random.fold_in(key, axis), (), 0, length) for axis, length in enumerate(result.shape)]
    longest = result.shape.index(max(result.shape))
    neighbour = spot[:longest] + [(spot[longest] + 1) % result.shape[longest]] + spot[longest + 1:]
    return result.at[tuple(spot)].set(low).at[tuple(neighbour)].set(largest)


def shard_levels(rng, dims, pieces, least, top_value):
    def one(axis_at, shards_of):
        steps = jax.random.uniform(jax.random.fold_in(jax.random.fold_in(rng, 6), axis_at), (shards_of,), jnp.float32, least / len(pieces), top_value / len(pieces))
        return jnp.repeat(jnp.exp(steps), dims[axis_at] // shards_of).reshape((-1,) + (1,) * (len(dims) - axis_at - 1))

    factor_of = one(*pieces[0])
    for cut in pieces[1:]:
        factor_of = factor_of * one(*cut)
    return factor_of


def gaussian(rng, dims, deviation, limit, pieces=(), kind=jnp.bfloat16):
    array = jax.random.normal(rng, dims, jnp.float32) * deviation
    if len(pieces) > 0:
        array = shard_levels(rng, dims, pieces, -0.22, 0.18) * array
    return jnp.clip(array, min=-limit, max=limit).astype(kind)


def setup_inputs(seed: int = 0) -> dict:
    keys = jax.random.split(jax.random.key(seed), 5)
    inputs = gaussian(keys[0], (MICRO, TOKENS, D), 1.0, 6.0, ((1, 8),))
    weights = gaussian(keys[1], (N_SEGMENT, D, D), (D // 2) ** -0.5, 0.09375, ((0, 4), (2, 8)))
    keep_mask = place_ends((jax.random.randint(keys[2], (N_SEGMENT, D // BLK, D // BLK), 0, 2) < 1).astype(jnp.int32), jax.random.fold_in(keys[2], 1), 0, 1)
    gains = jnp.clip(1.0 + 0.18 * jax.random.normal(keys[3], (N_SEGMENT, D), jnp.float32), 0.1, 1.9)
    return dict(inputs=inputs, weights=weights, keep_mask=keep_mask, gains=gains)


norm_eps = 1e-05
damp_share = 0.25

def reference(inputs, weights, keep_mask, gains):
    layer_in = inputs.reshape(MICRO * TOKENS, D)
    count = MICRO * TOKENS
    act_list = []
    factor_list = []
    for segment_num in range(N_SEGMENT):
        group_cols = layer_in[:, :GRP]
        gram = lax.dot_general(group_cols.astype(jnp.float32), group_cols.astype(jnp.float32), (((0,), (0,)), ((), ())), preferred_element_type=jnp.float32)
        hess = gram / count
        damp_val = damp_share * jnp.mean(jnp.diagonal(hess))
        hess = hess + damp_val * jnp.eye(GRP, dtype=jnp.float32)
        factor_list.append(jnp.linalg.cholesky(hess).T)
        block_mask = keep_mask[segment_num].astype(jnp.bfloat16)
        nblk = D // BLK
        pruned = (weights[segment_num].reshape(nblk, BLK, nblk, BLK) * block_mask[:, None, :, None]).reshape(D, D)
        row_vals = layer_in.astype(jnp.float32)
        mean_sq = lax.optimization_barrier(jnp.mean(row_vals * row_vals, axis=-1, keepdims=True))
        normed = (row_vals * lax.rsqrt(mean_sq + norm_eps) * gains[segment_num][None, :]).astype(jnp.bfloat16)
        product = jnp.dot(normed.astype(jnp.float32), pruned.astype(jnp.float32), preferred_element_type=jnp.float32)
        layer_out = (row_vals + product).astype(jnp.bfloat16)
        act_list.append(layer_out.reshape(MICRO, TOKENS, D))
        layer_in = layer_out
    return (jnp.stack(act_list), jnp.stack(factor_list))
```

```python
import functools

import jax
import jax.numpy as jnp
from jax import lax
from jax.experimental import pallas as pl
from jax.experimental.pallas import tpu as pltpu
from jax.sharding import PartitionSpec as P

GRP = 1024
LANES = 128
RANK_MAX = 64


norm_eps = 1e-05
damp_share = 0.25


def parts3(value):
    high = value.astype(jnp.bfloat16)
    rest = value - high.astype(jnp.float32)
    mid = rest.astype(jnp.bfloat16)
    low = (rest - mid.astype(jnp.float32)).astype(jnp.bfloat16)
    return jnp.concatenate([high, mid, low], axis=0)


def factor_kernel(x_ref, out_ref, perm_ref, y_ref, a_ref, row_ref, w_ref):
    rank, size = x_ref.shape
    steps = size // LANES
    f32 = jnp.float32
    for m in range(steps):
        col = lax.broadcasted_iota(jnp.int32, (size, LANES), 0)
        run = lax.broadcasted_iota(jnp.int32, (size, LANES), 1)
        perm_ref[:, m * LANES:(m + 1) * LANES] = jnp.where(col == run * steps + m, 1.0, 0.0).astype(jnp.bfloat16)
    x = x_ref[...]
    y = jnp.dot(x, perm_ref[...], preferred_element_type=f32)
    for m in range(steps):
        y_ref[m] = y[:, m * LANES:(m + 1) * LANES]
    mu = (damp_share / size) * jnp.sum(jnp.sum(y * y, axis=0, keepdims=True), axis=1, keepdims=True)
    for i in range(rank):
        acc = y_ref[0, pl.ds(i, 1), :] * y_ref[0]
        for m in range(1, steps):
            acc = acc + y_ref[m, pl.ds(i, 1), :] * y_ref[m]
        a_ref[i] = acc
    before = lax.broadcasted_iota(jnp.int32, (LANES, LANES), 0) < lax.broadcasted_iota(jnp.int32, (LANES, LANES), 1)
    prefix = jnp.dot(
        a_ref[...].reshape(rank * rank, LANES),
        before.astype(f32),
        precision=lax.Precision.HIGHEST,
        preferred_element_type=f32,
    ).reshape(rank, rank, LANES)
    sub = lax.broadcasted_iota(jnp.int32, (rank, LANES), 0)
    inv_mu = 1.0 / mu
    for i in range(rank):
        a_ref[i] = prefix[i] * inv_mu + jnp.where(sub == i, 1.0, 0.0)

    def sweep(p, carry):
        row_ref[0] = a_ref[p]
        inv_d = 1.0 / row_ref[0, pl.ds(p, 1), :]
        scaled = row_ref[0] * inv_d
        row_ref[1] = scaled
        at = sub == p
        for i in range(rank):
            a_ref[i] = jnp.where(at, row_ref[1, pl.ds(i, 1), :], a_ref[i] - row_ref[0, pl.ds(i, 1), :] * scaled)
        a_ref[p] = jnp.where(at, -inv_d, scaled)
        return carry

    lax.fori_loop(0, rank, sweep, 0)
    unit = rank ** -0.5
    for m in range(steps):
        v = y_ref[m]
        u = -a_ref[0] * y_ref[m, pl.ds(0, 1), :]
        for j in range(1, rank):
            u = u - a_ref[j] * y_ref[m, pl.ds(j, 1), :]
        d = mu + jnp.sum(v * u, axis=0, keepdims=True)
        inv_root = 1.0 / jnp.sqrt(d)
        g = u * inv_root
        lanes = pl.ds(m * LANES, LANES)
        w_ref[pl.ds(0, rank), lanes] = g * unit
        w_ref[pl.ds(rank, 8), lanes] = jnp.broadcast_to(mu * inv_root * unit, (8, LANES))
        if m < steps - 1:
            row_ref[0] = g
            for i in range(rank):
                a_ref[i] = a_ref[i] + row_ref[0, pl.ds(i, 1), :] * g
    natural = lax.dot_general(
        parts3(w_ref[...]), perm_ref[...], (((1,), (1,)), ((), ())), preferred_element_type=f32
    )
    tall = rank + 8
    diag = sum(natural[p * tall + rank:p * tall + rank + 1] for p in range(3))
    left = jnp.concatenate([natural[p * tall:p * tall + rank] for p in range(3)], axis=0).astype(jnp.bfloat16)
    right = jnp.concatenate([x, x, x], axis=0)
    for b in range(steps):
        lo = b * LANES
        block = lax.dot_general(
            left[:, lo:lo + LANES], right[:, lo:], (((0,), (0,)), ((), ())), preferred_element_type=f32
        )
        here = lax.broadcasted_iota(jnp.int32, (LANES, size - lo), 0)
        there = lax.broadcasted_iota(jnp.int32, (LANES, size - lo), 1)
        kept = jnp.where(there > here, block, 0.0)
        out_ref[pl.ds(lo, LANES), pl.ds(lo, size - lo)] = jnp.where(there == here, block + diag[:, lo:], kept)
        if b:
            out_ref[pl.ds(lo, LANES), pl.ds(0, lo)] = jnp.zeros((LANES, lo), f32)


def damped_factor(rows):
    rank, size = rows.shape
    if rank > RANK_MAX or rank % 16 or size % LANES:
        gram = lax.dot_general(rows, rows, (((0,), (0,)), ((), ())), preferred_element_type=jnp.float32)
        hess = gram / rank
        hess = hess + damp_share * jnp.mean(jnp.diagonal(hess)) * jnp.eye(size, dtype=jnp.float32)
        return jnp.linalg.cholesky(hess).T
    return pl.pallas_call(
        factor_kernel,
        out_shape=jax.ShapeDtypeStruct((size, size), jnp.float32),
        in_specs=[pl.BlockSpec(memory_space=pltpu.VMEM)],
        out_specs=pl.BlockSpec(memory_space=pltpu.VMEM),
        scratch_shapes=[
            pltpu.VMEM((size, size), jnp.bfloat16),
            pltpu.VMEM((size // LANES, rank, LANES), jnp.float32),
            pltpu.VMEM((rank, rank, LANES), jnp.float32),
            pltpu.VMEM((2, rank, LANES), jnp.float32),
            pltpu.VMEM((rank + 8, size), jnp.float32),
        ],
        compiler_params=pltpu.CompilerParams(vmem_limit_bytes=24 * 2**20),
        name="factor",
    )(rows)


def shifted(value, axis, by):
    devices = lax.axis_size(axis)
    pairs = [(i, i + by) for i in range(devices) if 0 <= i + by < devices]
    return lax.ppermute(value, axis, pairs)


def local(inputs, weights, keep_mask, gains):
    segment_count = lax.axis_size("segment")
    segment_idx = lax.axis_index("segment")
    tok_idx = lax.axis_index("tok")
    micro_count, row_count, width = inputs.shape
    col_width = weights.shape[2]
    nblk = keep_mask.shape[1]
    blk_size = width // nblk
    col_blocks = keep_mask.shape[2]
    block_mask = keep_mask[0].astype(jnp.bfloat16)
    pruned = (
        weights[0].reshape(nblk, blk_size, col_blocks, blk_size) * block_mask[:, None, :, None]
    ).reshape(width, col_width)
    gain_row = gains[0][None, :]
    col_start = tok_idx * col_width
    current = inputs.reshape(micro_count * row_count, width)
    stored = jnp.zeros_like(current)
    group = None
    for tick_num in range(segment_count):
        mine = segment_idx == tick_num
        whole = lax.all_gather(current, "tok", axis=0, tiled=True)
        group_now = whole[:, :GRP]
        group = group_now if group is None else jnp.where(mine, group_now, group)
        row_vals = whole.astype(jnp.float32)
        mean_sq = jnp.mean(row_vals * row_vals, axis=-1, keepdims=True)
        normed = (row_vals * lax.rsqrt(mean_sq + norm_eps) * gain_row).astype(jnp.bfloat16)
        product = jnp.dot(normed, pruned, preferred_element_type=jnp.float32)
        resid_cols = lax.dynamic_slice_in_dim(row_vals, col_start, col_width, 1)
        new_cols = (resid_cols + product).astype(jnp.bfloat16)
        output = lax.all_to_all(new_cols, "tok", split_axis=0, concat_axis=1, tiled=True)
        stored = jnp.where(mine, output, stored)
        if tick_num < segment_count - 1:
            current = shifted(output, "segment", 1)
    return (stored.reshape((1,) + inputs.shape), damped_factor(group)[None])


def solution(mesh):
    return jax.shard_map(
        local,
        mesh=mesh,
        in_specs=(
            P(None, "tok", None),
            P("segment", None, "tok"),
            P("segment", None, "tok"),
            P("segment", None),
        ),
        out_specs=(P("segment", None, "tok", None), P("segment", None, None)),
        check_vma=False,
    )
```

```python
import functools

import jax
import jax.numpy as jnp
from jax import lax
from jax.experimental import pallas as pl
from jax.experimental.pallas import tpu as pltpu
from jax.sharding import PartitionSpec as P

GRP = 1024
LANES = 128
RANK_MAX = 64


norm_eps = 1e-05
damp_share = 0.25


def parts3(value):
    high = value.astype(jnp.bfloat16)
    rest = value - high.astype(jnp.float32)
    mid = rest.astype(jnp.bfloat16)
    low = (rest - mid.astype(jnp.float32)).astype(jnp.bfloat16)
    return jnp.concatenate([high, mid, low], axis=0)


def factor_kernel(x_ref, out_ref, perm_ref, y_ref, a_ref, row_ref, w_ref):
    rank, size = x_ref.shape
    steps = size // LANES
    f32 = jnp.float32
    for m in range(steps):
        col = lax.broadcasted_iota(jnp.int32, (size, LANES), 0)
        run = lax.broadcasted_iota(jnp.int32, (size, LANES), 1)
        perm_ref[:, m * LANES:(m + 1) * LANES] = jnp.where(col == run * steps + m, 1.0, 0.0).astype(jnp.bfloat16)
    x = x_ref[...]
    y = jnp.dot(x, perm_ref[...], preferred_element_type=f32)
    for m in range(steps):
        y_ref[m] = y[:, m * LANES:(m + 1) * LANES]
    mu = (damp_share / size) * jnp.sum(jnp.sum(y * y, axis=0, keepdims=True), axis=1, keepdims=True)
    for i in range(rank):
        acc = y_ref[0, pl.ds(i, 1), :] * y_ref[0]
        for m in range(1, steps):
            acc = acc + y_ref[m, pl.ds(i, 1), :] * y_ref[m]
        a_ref[i] = acc
    before = lax.broadcasted_iota(jnp.int32, (LANES, LANES), 0) < lax.broadcasted_iota(jnp.int32, (LANES, LANES), 1)
    prefix = jnp.dot(
        a_ref[...].reshape(rank * rank, LANES),
        before.astype(f32),
        precision=lax.Precision.HIGHEST,
        preferred_element_type=f32,
    ).reshape(rank, rank, LANES)
    sub = lax.broadcasted_iota(jnp.int32, (rank, LANES), 0)
    inv_mu = 1.0 / mu
    for i in range(rank):
        a_ref[i] = prefix[i] * inv_mu + jnp.where(sub == i, 1.0, 0.0)

    def sweep(p, carry):
        row_ref[0] = a_ref[p]
        inv_d = 1.0 / row_ref[0, pl.ds(p, 1), :]
        scaled = row_ref[0] * inv_d
        row_ref[1] = scaled
        at = sub == p
        for i in range(rank):
            a_ref[i] = jnp.where(at, row_ref[1, pl.ds(i, 1), :], a_ref[i] - row_ref[0, pl.ds(i, 1), :] * scaled)
        a_ref[p] = jnp.where(at, -inv_d, scaled)
        return carry

    lax.fori_loop(0, rank, sweep, 0)
    unit = rank ** -0.5
    for m in range(steps):
        v = y_ref[m]
        u = -a_ref[0] * y_ref[m, pl.ds(0, 1), :]
        for j in range(1, rank):
            u = u - a_ref[j] * y_ref[m, pl.ds(j, 1), :]
        d = mu + jnp.sum(v * u, axis=0, keepdims=True)
        inv_root = 1.0 / jnp.sqrt(d)
        g = u * inv_root
        lanes = pl.ds(m * LANES, LANES)
        w_ref[pl.ds(0, rank), lanes] = g * unit
        w_ref[pl.ds(rank, 8), lanes] = jnp.broadcast_to(mu * inv_root * unit, (8, LANES))
        if m < steps - 1:
            row_ref[0] = g
            for i in range(rank):
                a_ref[i] = a_ref[i] + row_ref[0, pl.ds(i, 1), :] * g
    natural = lax.dot_general(
        parts3(w_ref[...]), perm_ref[...], (((1,), (1,)), ((), ())), preferred_element_type=f32
    )
    tall = rank + 8
    diag = sum(natural[p * tall + rank:p * tall + rank + 1] for p in range(3))
    left = jnp.concatenate([natural[p * tall:p * tall + rank] for p in range(3)], axis=0).astype(jnp.bfloat16)
    right = jnp.concatenate([x, x, x], axis=0)
    for b in range(steps):
        lo = b * LANES
        block = lax.dot_general(
            left[:, lo:lo + LANES], right[:, lo:], (((0,), (0,)), ((), ())), preferred_element_type=f32
        )
        here = lax.broadcasted_iota(jnp.int32, (LANES, size - lo), 0)
        there = lax.broadcasted_iota(jnp.int32, (LANES, size - lo), 1)
        kept = jnp.where(there > here, block, 0.0)
        out_ref[pl.ds(lo, LANES), pl.ds(lo, size - lo)] = jnp.where(there == here, block + diag[:, lo:], kept)
        if b:
            out_ref[pl.ds(lo, LANES), pl.ds(0, lo)] = jnp.zeros((LANES, lo), f32)


def damped_factor(rows):
    rank, size = rows.shape
    if rank > RANK_MAX or rank % 16 or size % LANES:
        gram = lax.dot_general(rows, rows, (((0,), (0,)), ((), ())), preferred_element_type=jnp.float32)
        hess = gram / rank
        hess = hess + damp_share * jnp.mean(jnp.diagonal(hess)) * jnp.eye(size, dtype=jnp.float32)
        return jnp.linalg.cholesky(hess).T
    return pl.pallas_call(
        factor_kernel,
        out_shape=jax.ShapeDtypeStruct((size, size), jnp.float32),
        in_specs=[pl.BlockSpec(memory_space=pltpu.VMEM)],
        out_specs=pl.BlockSpec(memory_space=pltpu.VMEM),
        scratch_shapes=[
            pltpu.VMEM((size, size), jnp.bfloat16),
            pltpu.VMEM((size // LANES, rank, LANES), jnp.float32),
            pltpu.VMEM((rank, rank, LANES), jnp.float32),
            pltpu.VMEM((2, rank, LANES), jnp.float32),
            pltpu.VMEM((rank + 8, size), jnp.float32),
        ],
        compiler_params=pltpu.CompilerParams(vmem_limit_bytes=24 * 2**20),
        name="factor",
    )(rows)


def shifted(value, axis, by):
    devices = lax.axis_size(axis)
    pairs = [(i, i + by) for i in range(devices) if 0 <= i + by < devices]
    return lax.ppermute(value, axis, pairs)


def local_xla(inputs, weights, keep_mask, gains):
    segment_count = lax.axis_size("segment")
    segment_idx = lax.axis_index("segment")
    tok_idx = lax.axis_index("tok")
    micro_count, row_count, width = inputs.shape
    col_width = weights.shape[2]
    nblk = keep_mask.shape[1]
    blk_size = width // nblk
    col_blocks = keep_mask.shape[2]
    block_mask = keep_mask[0].astype(jnp.bfloat16)
    pruned = (
        weights[0].reshape(nblk, blk_size, col_blocks, blk_size) * block_mask[:, None, :, None]
    ).reshape(width, col_width)
    gain_row = gains[0][None, :]
    col_start = tok_idx * col_width
    current = inputs.reshape(micro_count * row_count, width)
    stored = jnp.zeros_like(current)
    group = None
    for tick_num in range(segment_count):
        mine = segment_idx == tick_num
        whole = lax.all_gather(current, "tok", axis=0, tiled=True)
        group_now = whole[:, :GRP]
        group = group_now if group is None else jnp.where(mine, group_now, group)
        row_vals = whole.astype(jnp.float32)
        mean_sq = jnp.mean(row_vals * row_vals, axis=-1, keepdims=True)
        normed = (row_vals * lax.rsqrt(mean_sq + norm_eps) * gain_row).astype(jnp.bfloat16)
        product = jnp.dot(normed, pruned, preferred_element_type=jnp.float32)
        resid_cols = lax.dynamic_slice_in_dim(row_vals, col_start, col_width, 1)
        new_cols = (resid_cols + product).astype(jnp.bfloat16)
        output = lax.all_to_all(new_cols, "tok", split_axis=0, concat_axis=1, tiled=True)
        stored = jnp.where(mine, output, stored)
        if tick_num < segment_count - 1:
            current = shifted(output, "segment", 1)
    return (stored.reshape((1,) + inputs.shape), damped_factor(group)[None])

def forward_kernel(
    x_in, w_hbm, keep, gain, acts, group,
    w_buf, x_buf, rows_buf, rows_f32, mask_row, acc, sq_sum, y_send, y_rows, out_rows,
    w_sem, next_send, x_recv, relay_send, a_send, a_recv,
):
    f32 = jnp.float32
    segments, toks = lax.axis_size("segment"), lax.axis_size("tok")
    seg, tok = lax.axis_index("segment"), lax.axis_index("tok")
    pairs = toks // 2
    pair, core = tok // 2, tok % 2
    sister = tok + 1 - 2 * core
    micro, piece, width = x_in.shape
    _, rows, cols = x_buf.shape
    nblk, col_blocks = keep.shape[1:]
    blk = width // nblk
    per_chunk = nblk // toks

    def place(step, which):
        return lax.rem(pair + step, pairs) * 2 + which

    def remote(src, dst, send, recv, to_seg, to_tok):
        return pltpu.make_async_remote_copy(
            src_ref=src, dst_ref=dst, send_sem=send, recv_sem=recv,
            device_id=(to_seg, to_tok), device_id_type=pl.DeviceIdType.MESH,
        )

    def w_copy(k):
        return pltpu.make_async_copy(w_hbm.at[0, pl.ds(k * cols, cols), :], w_buf.at[k], w_sem.at[k])

    for k in range(toks):
        w_copy(k).start()

    barrier = pltpu.get_barrier_semaphore()

    def greet(to_seg, to_tok):
        pl.semaphore_signal(barrier, inc=1, device_id=(to_seg, to_tok), device_id_type=pl.DeviceIdType.MESH)

    for k in range(1, toks):
        greet(seg, lax.rem(tok + k, toks))

    @pl.when(seg > 0)
    def _():
        for k in range(pairs):
            greet(seg - 1, place(k, core))

    @pl.when(seg < segments - 1)
    def _():
        for k in range(pairs):
            greet(seg + 1, place(k, core))

    before = jnp.where(seg > 0, pairs, 0)
    after = jnp.where(seg < segments - 1, pairs, 0)
    pl.semaphore_wait(barrier, toks - 1 + before + after)

    def first_copy(k):
        to = sister if k == 0 else place(k, core)
        return remote(x_in, rows_buf.at[tok], next_send.at[k], x_recv.at[tok], seg, to)

    @pl.when(seg == 0)
    def _():
        for k in range(pairs):
            first_copy(k).start()

    spread = lax.broadcasted_iota(jnp.int32, (col_blocks, cols), 1) // blk
    spread = jnp.where(spread == lax.broadcasted_iota(jnp.int32, (col_blocks, cols), 0), 1.0, 0.0)
    mask_row[...] = jnp.dot(
        keep[0].astype(f32).astype(jnp.bfloat16), spread.astype(jnp.bfloat16), preferred_element_type=f32
    )

    def prune(k, carry):
        w_copy(k).wait()
        for b in range(per_chunk):
            kept = jnp.broadcast_to(mask_row[pl.ds(k * per_chunk + b, 1), :], (16, cols)).astype(jnp.bfloat16)
            block = w_buf[k, pl.ds(b * blk, blk), :].reshape(blk // 16, 16, cols)
            w_buf[k, pl.ds(b * blk, blk), :] = (block * kept[None]).reshape(blk, cols)
        return carry

    lax.fori_loop(0, toks, prune, 0)
    acc[...] = jnp.zeros_like(acc)
    sq_sum[...] = jnp.zeros_like(sq_sum)

    def relay(buf, k, src):
        return remote(buf.at[src], buf.at[src], relay_send.at[k], x_recv.at[src], seg, sister)

    def step(src):
        x = x_buf[src].astype(f32)
        sq = x * x
        part = sq[:, :LANES]
        for lo in range(LANES, cols, LANES):
            part = part + sq[:, lo:lo + LANES]
        sq_sum[...] += part
        gained = (x * gain[0:1, pl.ds(pl.multiple_of(src * cols, cols), cols)]).astype(jnp.bfloat16)
        acc[...] += jnp.dot(gained, w_buf[src], preferred_element_type=f32)

    @pl.when(seg == 0)
    def _():
        rows_buf[tok] = x_in[...]
        for k in range(1, pairs):
            src = place(pairs - k, core)
            relay(rows_buf, k, src).wait_recv()
            relay(rows_buf, k, src).start()
        for k in range(pairs):
            relay(rows_buf, k, place(pairs - k, 1 - core)).wait_recv()
        for t in range(toks):
            for m in range(micro):
                rows_f32[pl.ds((t * micro + m) * piece, piece), :] = rows_buf[t, m].astype(f32)
        for t in range(toks):
            x_buf[t] = rows_f32[:, t * cols:(t + 1) * cols].astype(jnp.bfloat16)

        def one(src, carry):
            step(src)
            return carry

        lax.fori_loop(0, toks, one, 0)
        for k in range(pairs):
            first_copy(k).wait_send()
        for k in range(1, pairs):
            relay(rows_buf, k, place(pairs - k, core)).wait_send()

    @pl.when(seg > 0)
    def _():
        def direct(k, carry):
            src = place(k, core)
            relay(x_buf, k, src).wait_recv()
            relay(x_buf, k, src).start()
            step(src)
            return carry

        lax.fori_loop(0, pairs, direct, 0)

        def relayed(k, carry):
            src = place(k, 1 - core)
            relay(x_buf, k, src).wait_recv()
            step(src)
            return carry

        lax.fori_loop(0, pairs, relayed, 0)
        for k in range(pairs):
            relay(x_buf, k, place(k, core)).wait_send()

    mean_sq = jnp.sum(sq_sum[...], axis=1, keepdims=True) * (1.0 / width)
    y = x_buf[tok].astype(f32) + acc[...] * lax.rsqrt(mean_sq + norm_eps)
    y_send[...] = y.astype(jnp.bfloat16)

    def next_copy(k):
        return remote(y_send, x_buf.at[tok], next_send.at[k], x_recv.at[tok], seg + 1, place(k, core))

    @pl.when(seg < segments - 1)
    def _():
        for k in range(pairs):
            next_copy(k).start()

    acc[...] = y
    for t in range(toks):
        for m in range(micro):
            y_rows[t, m] = acc[pl.ds((t * micro + m) * piece, piece), :].astype(jnp.bfloat16)

    def a_copy(k):
        to = lax.rem(tok + k, toks)
        return remote(y_rows.at[to], out_rows.at[tok], a_send.at[k], a_recv.at[tok], seg, to)

    for k in range(1, toks):
        a_copy(k).start()
    for t in range(group.shape[1] // cols):
        group[:, t * cols:(t + 1) * cols] = x_buf[t]
    out_rows[tok] = y_rows[tok]
    for k in range(1, toks):
        src = lax.rem(tok + toks - k, toks)
        remote(y_rows.at[src], out_rows.at[src], a_send.at[k], a_recv.at[src], seg, src).wait_recv()
    for t in range(toks):
        acts[0, :, :, t * cols:(t + 1) * cols] = out_rows[t]
    for k in range(1, toks):
        a_copy(k).wait_send()

    @pl.when(seg < segments - 1)
    def _():
        for k in range(pairs):
            next_copy(k).wait_send()


def local_kernel(inputs, weights, keep_mask, gains):
    toks = lax.axis_size("tok")
    micro, piece, width = inputs.shape
    cols = weights.shape[2]
    nblk = keep_mask.shape[1]
    rows = micro * piece * toks
    vmem = pl.BlockSpec(memory_space=pltpu.VMEM)
    bf16, f32 = jnp.bfloat16, jnp.float32
    dma = pltpu.SemaphoreType.DMA
    acts, group = pl.pallas_call(
        forward_kernel,
        out_shape=(
            jax.ShapeDtypeStruct((1,) + inputs.shape, bf16),
            jax.ShapeDtypeStruct((rows, min(GRP, width)), bf16),
        ),
        in_specs=[vmem, pl.BlockSpec(memory_space=pltpu.HBM), vmem, vmem],
        out_specs=(vmem, vmem),
        scratch_shapes=[
            pltpu.VMEM((toks, width // toks, cols), bf16),
            pltpu.VMEM((toks, rows, cols), bf16),
            pltpu.VMEM((toks, micro, piece, width), bf16),
            pltpu.VMEM((rows, width), f32),
            pltpu.VMEM((nblk, cols), f32),
            pltpu.VMEM((rows, cols), f32),
            pltpu.VMEM((rows, LANES), f32),
            pltpu.VMEM((rows, cols), bf16),
            pltpu.VMEM((toks, micro, piece, cols), bf16),
            pltpu.VMEM((toks, micro, piece, cols), bf16),
            dma((toks,)), dma((toks,)), dma((toks,)), dma((toks,)), dma((toks,)), dma((toks,)),
        ],
        compiler_params=pltpu.CompilerParams(
            collective_id=0, has_side_effects=True, vmem_limit_bytes=48 * 2**20
        ),
        name="forward",
    )(inputs, weights, keep_mask, gains)
    return (acts, damped_factor(group)[None])


def local(inputs, weights, keep_mask, gains):
    toks = lax.axis_size("tok")
    rows = inputs.shape[0] * inputs.shape[1] * toks
    width, cols = weights.shape[1:]
    if rows > RANK_MAX or rows % 16 or toks % 2 or cols % LANES or GRP % cols:
        return local_xla(inputs, weights, keep_mask, gains)
    return local_kernel(inputs, weights, keep_mask, gains)


def solution(mesh):
    return jax.shard_map(
        local,
        mesh=mesh,
        in_specs=(
            P(None, "tok", None),
            P("segment", None, "tok"),
            P("segment", None, "tok"),
            P("segment", None),
        ),
        out_specs=(P("segment", None, "tok", None), P("segment", None, None)),
        check_vma=False,
    )
```

```python
import functools

import jax
import jax.numpy as jnp
from jax import lax
from jax.experimental import pallas as pl
from jax.experimental.pallas import tpu as pltpu
from jax.sharding import PartitionSpec as P

GRP = 1024
LANES = 128
RANK_MAX = 64


norm_eps = 1e-05
damp_share = 0.25


def parts3(value):
    high = value.astype(jnp.bfloat16)
    rest = value - high.astype(jnp.float32)
    mid = rest.astype(jnp.bfloat16)
    low = (rest - mid.astype(jnp.float32)).astype(jnp.bfloat16)
    return jnp.concatenate([high, mid, low], axis=0)


def factor_kernel(x_ref, out_ref, perm_ref, y_ref, a_ref, row_ref, w_ref):
    rank, size = x_ref.shape
    steps = size // LANES
    f32 = jnp.float32
    for m in range(steps):
        col = lax.broadcasted_iota(jnp.int32, (size, LANES), 0)
        run = lax.broadcasted_iota(jnp.int32, (size, LANES), 1)
        perm_ref[:, m * LANES:(m + 1) * LANES] = jnp.where(col == run * steps + m, 1.0, 0.0).astype(jnp.bfloat16)
    x = x_ref[...]
    y = jnp.dot(x, perm_ref[...], preferred_element_type=f32)
    for m in range(steps):
        y_ref[m] = y[:, m * LANES:(m + 1) * LANES]
    mu = (damp_share / size) * jnp.sum(jnp.sum(y * y, axis=0, keepdims=True), axis=1, keepdims=True)
    for i in range(rank):
        acc = y_ref[0, pl.ds(i, 1), :] * y_ref[0]
        for m in range(1, steps):
            acc = acc + y_ref[m, pl.ds(i, 1), :] * y_ref[m]
        a_ref[i] = acc
    before = lax.broadcasted_iota(jnp.int32, (LANES, LANES), 0) < lax.broadcasted_iota(jnp.int32, (LANES, LANES), 1)
    prefix = jnp.dot(
        a_ref[...].reshape(rank * rank, LANES),
        before.astype(f32),
        precision=lax.Precision.HIGHEST,
        preferred_element_type=f32,
    ).reshape(rank, rank, LANES)
    sub = lax.broadcasted_iota(jnp.int32, (rank, LANES), 0)
    inv_mu = 1.0 / mu
    for i in range(rank):
        a_ref[i] = prefix[i] * inv_mu + jnp.where(sub == i, 1.0, 0.0)

    def sweep(p, carry):
        row_ref[0] = a_ref[p]
        inv_d = 1.0 / row_ref[0, pl.ds(p, 1), :]
        scaled = row_ref[0] * inv_d
        row_ref[1] = scaled
        at = sub == p
        for i in range(rank):
            a_ref[i] = jnp.where(at, row_ref[1, pl.ds(i, 1), :], a_ref[i] - row_ref[0, pl.ds(i, 1), :] * scaled)
        a_ref[p] = jnp.where(at, -inv_d, scaled)
        return carry

    lax.fori_loop(0, rank, sweep, 0)
    unit = rank ** -0.5
    for m in range(steps):
        v = y_ref[m]
        u = -a_ref[0] * y_ref[m, pl.ds(0, 1), :]
        for j in range(1, rank):
            u = u - a_ref[j] * y_ref[m, pl.ds(j, 1), :]
        d = mu + jnp.sum(v * u, axis=0, keepdims=True)
        inv_root = 1.0 / jnp.sqrt(d)
        g = u * inv_root
        lanes = pl.ds(m * LANES, LANES)
        w_ref[pl.ds(0, rank), lanes] = g * unit
        w_ref[pl.ds(rank, 8), lanes] = jnp.broadcast_to(mu * inv_root * unit, (8, LANES))
        if m < steps - 1:
            row_ref[0] = g
            for i in range(rank):
                a_ref[i] = a_ref[i] + row_ref[0, pl.ds(i, 1), :] * g
    natural = lax.dot_general(
        parts3(w_ref[...]), perm_ref[...], (((1,), (1,)), ((), ())), preferred_element_type=f32
    )
    tall = rank + 8
    diag = sum(natural[p * tall + rank:p * tall + rank + 1] for p in range(3))
    left = jnp.concatenate([natural[p * tall:p * tall + rank] for p in range(3)], axis=0).astype(jnp.bfloat16)
    right = jnp.concatenate([x, x, x], axis=0)
    for b in range(steps):
        lo = b * LANES
        block = lax.dot_general(
            left[:, lo:lo + LANES], right[:, lo:], (((0,), (0,)), ((), ())), preferred_element_type=f32
        )
        here = lax.broadcasted_iota(jnp.int32, (LANES, size - lo), 0)
        there = lax.broadcasted_iota(jnp.int32, (LANES, size - lo), 1)
        kept = jnp.where(there > here, block, 0.0)
        out_ref[pl.ds(lo, LANES), pl.ds(lo, size - lo)] = jnp.where(there == here, block + diag[:, lo:], kept)
        if b:
            out_ref[pl.ds(lo, LANES), pl.ds(0, lo)] = jnp.zeros((LANES, lo), f32)


def damped_factor(rows):
    rank, size = rows.shape
    if rank > RANK_MAX or rank % 16 or size % LANES:
        gram = lax.dot_general(rows, rows, (((0,), (0,)), ((), ())), preferred_element_type=jnp.float32)
        hess = gram / rank
        hess = hess + damp_share * jnp.mean(jnp.diagonal(hess)) * jnp.eye(size, dtype=jnp.float32)
        return jnp.linalg.cholesky(hess).T
    return pl.pallas_call(
        factor_kernel,
        out_shape=jax.ShapeDtypeStruct((size, size), jnp.float32),
        in_specs=[pl.BlockSpec(memory_space=pltpu.VMEM)],
        out_specs=pl.BlockSpec(memory_space=pltpu.VMEM),
        scratch_shapes=[
            pltpu.VMEM((size, size), jnp.bfloat16),
            pltpu.VMEM((size // LANES, rank, LANES), jnp.float32),
            pltpu.VMEM((rank, rank, LANES), jnp.float32),
            pltpu.VMEM((2, rank, LANES), jnp.float32),
            pltpu.VMEM((rank + 8, size), jnp.float32),
        ],
        compiler_params=pltpu.CompilerParams(vmem_limit_bytes=24 * 2**20),
        name="factor",
    )(rows)


def shifted(value, axis, by):
    devices = lax.axis_size(axis)
    pairs = [(i, i + by) for i in range(devices) if 0 <= i + by < devices]
    return lax.ppermute(value, axis, pairs)


def local_xla(inputs, weights, keep_mask, gains):
    segment_count = lax.axis_size("segment")
    segment_idx = lax.axis_index("segment")
    tok_idx = lax.axis_index("tok")
    micro_count, row_count, width = inputs.shape
    col_width = weights.shape[2]
    nblk = keep_mask.shape[1]
    blk_size = width // nblk
    col_blocks = keep_mask.shape[2]
    block_mask = keep_mask[0].astype(jnp.bfloat16)
    pruned = (
        weights[0].reshape(nblk, blk_size, col_blocks, blk_size) * block_mask[:, None, :, None]
    ).reshape(width, col_width)
    gain_row = gains[0][None, :]
    col_start = tok_idx * col_width
    current = inputs.reshape(micro_count * row_count, width)
    stored = jnp.zeros_like(current)
    group = None
    for tick_num in range(segment_count):
        mine = segment_idx == tick_num
        whole = lax.all_gather(current, "tok", axis=0, tiled=True)
        group_now = whole[:, :GRP]
        group = group_now if group is None else jnp.where(mine, group_now, group)
        row_vals = whole.astype(jnp.float32)
        mean_sq = jnp.mean(row_vals * row_vals, axis=-1, keepdims=True)
        normed = (row_vals * lax.rsqrt(mean_sq + norm_eps) * gain_row).astype(jnp.bfloat16)
        product = jnp.dot(normed, pruned, preferred_element_type=jnp.float32)
        resid_cols = lax.dynamic_slice_in_dim(row_vals, col_start, col_width, 1)
        new_cols = (resid_cols + product).astype(jnp.bfloat16)
        output = lax.all_to_all(new_cols, "tok", split_axis=0, concat_axis=1, tiled=True)
        stored = jnp.where(mine, output, stored)
        if tick_num < segment_count - 1:
            current = shifted(output, "segment", 1)
    return (stored.reshape((1,) + inputs.shape), damped_factor(group)[None])

def forward_kernel(
    x_in, w_hbm, keep, gain_hbm, acts, group, gain,
    w_buf, x_buf, rows_buf, rows_f32, mask_row, acc, sq_sum, y_send, y_rows, out_rows,
    in_sem, w_sem, next_send, x_recv, relay_send, a_send, a_recv,
):
    f32 = jnp.float32
    segments, toks = lax.axis_size("segment"), lax.axis_size("tok")
    seg, tok = lax.axis_index("segment"), lax.axis_index("tok")
    pairs = toks // 2
    pair, core = tok // 2, tok % 2
    sister = tok + 1 - 2 * core
    micro, piece, width = x_in.shape
    _, rows, cols = x_buf.shape
    nblk, col_blocks = keep.shape[1:]
    blk = width // nblk
    per_chunk = nblk // toks

    def place(step, which):
        return jnp.where(2 * pair >= pairs, step, pairs - 1 - step) * 2 + which

    def remote(src, dst, send, recv, to_seg, to_tok):
        return pltpu.make_async_remote_copy(
            src_ref=src, dst_ref=dst, send_sem=send, recv_sem=recv,
            device_id=(to_seg, to_tok), device_id_type=pl.DeviceIdType.MESH,
        )

    def w_copy(k):
        return pltpu.make_async_copy(w_hbm.at[0, pl.ds(k * cols, cols), :], w_buf.at[k], w_sem.at[k])

    own_rows = pltpu.make_async_copy(x_in, rows_buf.at[tok], in_sem.at[0])
    gain_copy = pltpu.make_async_copy(gain_hbm, gain, in_sem.at[1])
    gain_copy.start()

    @pl.when(seg == 0)
    def _():
        own_rows.start()

    for k in range(toks):
        w_copy(k).start()

    barrier = pltpu.get_barrier_semaphore()

    def greet(to_seg, to_tok):
        pl.semaphore_signal(barrier, inc=1, device_id=(to_seg, to_tok), device_id_type=pl.DeviceIdType.MESH)

    for k in range(1, toks):
        greet(seg, lax.rem(tok + k, toks))

    @pl.when(seg > 0)
    def _():
        for k in range(pairs):
            greet(seg - 1, place(k, core))

    @pl.when(seg < segments - 1)
    def _():
        for k in range(pairs):
            greet(seg + 1, place(k, core))

    before = jnp.where(seg > 0, pairs, 0)
    after = jnp.where(seg < segments - 1, pairs, 0)
    pl.semaphore_wait(barrier, toks - 1 + before + after)

    def first_copy(to):
        return remote(x_in, rows_buf.at[tok], next_send.at[to // 2], x_recv.at[tok], seg, to)

    def first_start(to):
        first_copy(to).start()

    def others(act):
        for k in range(pairs):
            @pl.when(place(k, core) != tok)
            def _():
                act(place(k, core))

    def own_sister():
        return remote(x_in, rows_buf.at[tok], next_send.at[pair], x_recv.at[tok], seg, sister)

    @pl.when(seg == 0)
    def _():
        others(first_start)
        own_sister().start()

    spread = lax.broadcasted_iota(jnp.int32, (col_blocks, cols), 1) // blk
    spread = jnp.where(spread == lax.broadcasted_iota(jnp.int32, (col_blocks, cols), 0), 1.0, 0.0)
    mask_row[...] = jnp.dot(
        keep[0].astype(f32).astype(jnp.bfloat16), spread.astype(jnp.bfloat16), preferred_element_type=f32
    )

    def prune(k, carry):
        w_copy(k).wait()
        for b in range(per_chunk):
            kept = jnp.broadcast_to(mask_row[pl.ds(k * per_chunk + b, 1), :], (16, cols)).astype(jnp.bfloat16)
            block = w_buf[k, pl.ds(b * blk, blk), :].reshape(blk // 16, 16, cols)
            w_buf[k, pl.ds(b * blk, blk), :] = (block * kept[None]).reshape(blk, cols)
        return carry

    lax.fori_loop(0, toks, prune, 0)
    acc[...] = jnp.zeros_like(acc)
    sq_sum[...] = jnp.zeros_like(sq_sum)

    def relay(buf, src):
        return remote(buf.at[src], buf.at[src], relay_send.at[src // 2], x_recv.at[src], seg, sister)

    def wide(src):
        return gain[0:1, pl.ds(pl.multiple_of(src * cols, cols), cols)]

    def square(x):
        sq = x * x
        part = sq[:, :LANES]
        for lo in range(LANES, cols, LANES):
            part = part + sq[:, lo:lo + LANES]
        sq_sum[...] += part

    def row_scale():
        mean_sq = jnp.sum(sq_sum[...], axis=1, keepdims=True) * (1.0 / width)
        return lax.rsqrt(mean_sq + norm_eps)

    def step(src):
        x = x_buf[src].astype(f32)
        square(x)
        gained = x * wide(src)
        high = gained.astype(jnp.bfloat16)
        low = (gained - high.astype(f32)).astype(jnp.bfloat16)
        both = jnp.dot(jnp.concatenate([high, low], axis=0), w_buf[src], preferred_element_type=f32)
        acc[...] += both[:rows] + both[rows:]

    gain_copy.wait()

    @pl.when(seg == 0)
    def _():
        def pass_on(src):
            relay(rows_buf, src).wait_recv()
            relay(rows_buf, src).start()

        others(pass_on)
        own_rows.wait()
        for k in range(pairs):
            relay(rows_buf, place(k, 1 - core)).wait_recv()
        for t in range(toks):
            for m in range(micro):
                rows_f32[pl.ds((t * micro + m) * piece, piece), :] = rows_buf[t, m].astype(f32)
        for t in range(toks):
            x = rows_f32[:, t * cols:(t + 1) * cols]
            square(x)
            x_buf[t] = x.astype(jnp.bfloat16)
        scale = row_scale()

        def one(src, carry):
            normed = (x_buf[src].astype(f32) * scale * wide(src)).astype(jnp.bfloat16)
            acc[...] += jnp.dot(normed, w_buf[src], preferred_element_type=f32)
            return carry

        lax.fori_loop(0, toks, one, 0)
        others(lambda to: first_copy(to).wait_send())
        own_sister().wait_send()
        others(lambda src: relay(rows_buf, src).wait_send())

    @pl.when(seg > 0)
    def _():
        def direct(k, carry):
            src = place(k, core)
            relay(x_buf, src).wait_recv()
            relay(x_buf, src).start()
            step(src)
            return carry

        lax.fori_loop(0, pairs, direct, 0)

        def relayed(k, carry):
            src = place(k, 1 - core)
            relay(x_buf, src).wait_recv()
            step(src)
            return carry

        lax.fori_loop(0, pairs, relayed, 0)
        for k in range(pairs):
            relay(x_buf, place(k, core)).wait_send()
        acc[...] = acc[...] * row_scale()

    y = x_buf[tok].astype(f32) + acc[...]
    y_send[...] = y.astype(jnp.bfloat16)

    def next_copy(k):
        return remote(y_send, x_buf.at[tok], next_send.at[k], x_recv.at[tok], seg + 1, place(k, core))

    @pl.when(seg < segments - 1)
    def _():
        for k in range(pairs):
            next_copy(k).start()

    acc[...] = y
    for t in range(toks):
        for m in range(micro):
            y_rows[t, m] = acc[pl.ds((t * micro + m) * piece, piece), :].astype(jnp.bfloat16)

    def a_copy(k):
        to = lax.rem(tok + k, toks)
        return remote(y_rows.at[to], out_rows.at[tok], a_send.at[k], a_recv.at[tok], seg, to)

    for k in range(1, toks):
        a_copy(k).start()
    for t in range(group.shape[1] // cols):
        group[:, t * cols:(t + 1) * cols] = x_buf[t]
    out_rows[tok] = y_rows[tok]
    for k in range(1, toks):
        src = lax.rem(tok + toks - k, toks)
        remote(y_rows.at[src], out_rows.at[src], a_send.at[k], a_recv.at[src], seg, src).wait_recv()
    for t in range(toks):
        acts[0, :, :, t * cols:(t + 1) * cols] = out_rows[t]
    for k in range(1, toks):
        a_copy(k).wait_send()

    @pl.when(seg < segments - 1)
    def _():
        for k in range(pairs):
            next_copy(k).wait_send()


def local_kernel(inputs, weights, keep_mask, gains):
    toks = lax.axis_size("tok")
    micro, piece, width = inputs.shape
    cols = weights.shape[2]
    nblk = keep_mask.shape[1]
    rows = micro * piece * toks
    vmem = pl.BlockSpec(memory_space=pltpu.VMEM)
    hbm = pl.BlockSpec(memory_space=pltpu.HBM)
    bf16, f32 = jnp.bfloat16, jnp.float32
    dma = pltpu.SemaphoreType.DMA
    acts, group = pl.pallas_call(
        forward_kernel,
        out_shape=(
            jax.ShapeDtypeStruct((1,) + inputs.shape, bf16),
            jax.ShapeDtypeStruct((rows, min(GRP, width)), bf16),
        ),
        in_specs=[hbm, hbm, vmem, hbm],
        out_specs=(vmem, vmem),
        scratch_shapes=[
            pltpu.VMEM((1, width), f32),
            pltpu.VMEM((toks, width // toks, cols), bf16),
            pltpu.VMEM((toks, rows, cols), bf16),
            pltpu.VMEM((toks, micro, piece, width), bf16),
            pltpu.VMEM((rows, width), f32),
            pltpu.VMEM((nblk, cols), f32),
            pltpu.VMEM((rows, cols), f32),
            pltpu.VMEM((rows, LANES), f32),
            pltpu.VMEM((rows, cols), bf16),
            pltpu.VMEM((toks, micro, piece, cols), bf16),
            pltpu.VMEM((toks, micro, piece, cols), bf16),
            dma((2,)), dma((toks,)), dma((toks,)), dma((toks,)), dma((toks,)), dma((toks,)), dma((toks,)),
        ],
        compiler_params=pltpu.CompilerParams(
            collective_id=0, has_side_effects=True, vmem_limit_bytes=48 * 2**20
        ),
        name="forward",
    )(inputs, weights, keep_mask, gains)
    return (acts, damped_factor(group)[None])


def local(inputs, weights, keep_mask, gains):
    toks = lax.axis_size("tok")
    rows = inputs.shape[0] * inputs.shape[1] * toks
    width, cols = weights.shape[1:]
    if rows > RANK_MAX or rows % 16 or toks % 2 or cols % LANES or GRP % cols:
        return local_xla(inputs, weights, keep_mask, gains)
    return local_kernel(inputs, weights, keep_mask, gains)


def solution(mesh):
    return jax.shard_map(
        local,
        mesh=mesh,
        in_specs=(
            P(None, "tok", None),
            P("segment", None, "tok"),
            P("segment", None, "tok"),
            P("segment", None),
        ),
        out_specs=(P("segment", None, "tok", None), P("segment", None, None)),
        check_vma=False,
    )
```
